32 devices in a mesh: batch: 8 (over z, x), th: 2 (over y), tw: 2 (over core).
Axes of the slice: x: 2, y: 2, z: 4, core: 2. Of those that a mesh axis runs over, the one named last changes fastest.
Arguments:
- images: bfloat16 [64, 24, 24, 768], P('batch', 'th', 'tw'), may hold values from -6 to 6
- valid_slots: int32 [64], P('batch'), may hold values 0 or 1
- region_ids: int32 [24, 24], P('th', 'tw'), may hold values from 0 to 3
- relative_index: int32 [144, 144], replicated, may hold values from 0 to 528
- entry_weight: bfloat16 [768, 2304], P(('batch', 'th', 'tw')), may hold values from -0.21875 to 0.21875
- entry_bias: bfloat16 [1536], P(('batch', 'th', 'tw')), may hold values from -2 to 2
- exit_weight: bfloat16 [768, 768], P(('batch', 'th', 'tw')), may hold values from -1 to 1
- exit_bias: bfloat16 [768], P(('batch', 'th', 'tw')), may hold values from -2 to 2
- expand_weight: bfloat16 [768, 3072], P(('batch', 'th', 'tw')), may hold values from -0.21875 to 0.21875
- expand_bias: bfloat16 [3072], P(('batch', 'th', 'tw')), may hold values from -2 to 2
- reduce_weight: bfloat16 [3072, 768], P(('batch', 'th', 'tw')), may hold values from -0.109375 to 0.109375
- reduce_bias: bfloat16 [768], P(('batch', 'th', 'tw')), may hold values from -2 to 2
- first_gain: bfloat16 [768], P(('batch', 'th', 'tw')), may hold values from 0.099609375 to 1.8984375
- first_shift: bfloat16 [768], P(('batch', 'th', 'tw')), may hold values from -2 to 2
- second_gain: bfloat16 [768], P(('batch', 'th', 'tw')), may hold values from 0.099609375 to 1.8984375
- second_shift: bfloat16 [768], P(('batch', 'th', 'tw')), may hold values from -2 to 2
- bias_table: bfloat16 [529, 24], replicated, may hold values from -4 to 4
- cotangent: bfloat16 [64, 24, 24, 768], P('batch', 'th', 'tw'), may hold values from -6 to 6
Outputs:
- output: bfloat16 [64, 24, 24, 768], P('batch', 'th', 'tw')
- images_grad: bfloat16 [64, 24, 24, 768], P('batch', 'th', 'tw')
- entry_weight_grad: float32 [768, 2304], P(('batch', 'th', 'tw'))
- entry_bias_grad: float32 [1536], P(('batch', 'th', 'tw'))
- exit_weight_grad: float32 [768, 768], P(('batch', 'th', 'tw'))
- exit_bias_grad: float32 [768], P(('batch', 'th', 'tw'))
- expand_weight_grad: float32 [768, 3072], P(('batch', 'th', 'tw'))
- expand_bias_grad: float32 [3072], P(('batch', 'th', 'tw'))
- reduce_weight_grad: float32 [3072, 768], P(('batch', 'th', 'tw'))
- reduce_bias_grad: float32 [768], P(('batch', 'th', 'tw'))
- first_gain_grad: float32 [768], P(('batch', 'th', 'tw'))
- first_shift_grad: float32 [768], P(('batch', 'th', 'tw'))
- second_gain_grad: float32 [768], P(('batch', 'th', 'tw'))
- second_shift_grad: float32 [768], P(('batch', 'th', 'tw'))
- bias_table_grad: float32 [529, 24], replicated
The draws below stay inside these ranges and needn't reach their ends.
All inputs are finite; a program needn't handle non-finite values. No bound on the sum of `valid_slots` on one device may be relied on, other than what follows from the above.
Results may differ from the reference program's by a relative error of at most 0.013.
Values may be sent and summed in bfloat16 or wider, within the bound.
No kernel may reach another device: no remote copies, remote signals or barrier semaphores. Data moves between devices by JAX's collectives and lax.ppermute only.
A program may use at most 320 MiB of HBM per device.

```python
import math
import jax
import jax.numpy as jnp
from jax import lax

D = 768
HEADS = 24
HD = 32
FF = 3072
WIN = 12
SHIFT = 6
AREA = 144
TABLE = 529
HEIGHT = 24
WIDTH = 24
SLOTS = 64
N_TH = 2
N_TW = 2


def set_ends(values, stream_key, least, largest):
    spot = [jax.random.randint(jax.random.fold_in(stream_key, axis), (), 0, length) for axis, length in enumerate(values.shape)]
    main_axis = values.shape.index(max(values.shape))
    beside = spot[:main_axis] + [(spot[main_axis] + 1) % values.shape[main_axis]] + spot[main_axis + 1:]
    return values.at[tuple(spot)].set(least).at[tuple(beside)].set(largest)


def shard_levels(key, dims, cuts, low, largest):
    def one(position, shards_of):
        draws = jax.random.uniform(jax.random.fold_in(jax.random.fold_in(key, 6), position), (shards_of,), jnp.float32, low / len(cuts), largest / len(cuts))
        return jnp.repeat(jnp.exp(draws), dims[position] // shards_of).reshape((-1,) + (1,) * (len(dims) - position - 1))

    loudness = one(*cuts[0])
    for cut in cuts[1:]:
        loudness = loudness * one(*cut)
    return loudness


def normal_values(stream_key, extent, scale, limit, split=(), dtype=jnp.bfloat16):
    drawn = jax.random.normal(stream_key, extent, jnp.float32) * scale
    if len(split) > 0:
        drawn = shard_levels(stream_key, extent, split, -0.22, 0.18) * drawn
    return jnp.clip(drawn, min=-limit, max=limit).astype(dtype)


def setup_inputs(seed: int = 0) -> dict:
    splits = jax.random.split(jax.random.key(seed), 19)
    return {
        "images": normal_values(splits[0], (SLOTS, HEIGHT, WIDTH, D), 1.0, 6.0, ((0, 8), (1, 2), (2, 2))),
        "valid_slots": set_ends((jax.random.randint(splits[1], (SLOTS,), 0, 8) < 7).astype(jnp.int32), jax.random.fold_in(splits[1], 1), 0, 1),
        "region_ids": set_ends(jax.random.randint(splits[2], (HEIGHT, WIDTH), 0, 4), jax.random.fold_in(splits[2], 1), 0, 3).astype(jnp.int32),
        "relative_index": set_ends(jax.random.randint(splits[3], (AREA, AREA), 0, TABLE), jax.random.fold_in(splits[3], 1), 0, TABLE - 1).astype(jnp.int32),
        "entry_weight": normal_values(splits[4], (D, 3 * D), D ** -0.5, 0.21875, ((0, 32),)),
        "entry_bias": normal_values(splits[5], (2 * D,), 0.3, 2.0, ((0, 32),)),
        "exit_weight": normal_values(splits[6], (D, D), HD ** -0.5, 1.0, ((0, 32),)),
        "exit_bias": normal_values(splits[7], (D,), 0.3, 2.0, ((0, 32),)),
        "expand_weight": normal_values(splits[8], (D, FF), D ** -0.5, 0.21875, ((0, 32),)),
        "expand_bias": normal_values(splits[9], (FF,), 0.3, 2.0, ((0, 32),)),
        "reduce_weight": normal_values(splits[10], (FF, D), FF ** -0.5, 0.109375, ((0, 32),)),
        "reduce_bias": normal_values(splits[11], (D,), 0.3, 2.0, ((0, 32),)),
        "first_gain": jnp.clip(1.0 + 0.18 * jax.random.normal(splits[12], (D,), jnp.float32), 0.099609375, 1.8984375).astype(jnp.bfloat16),
        "first_shift": normal_values(splits[13], (D,), 0.3, 2.0, ((0, 32),)),
        "second_gain": jnp.clip(1.0 + 0.18 * jax.random.normal(splits[14], (D,), jnp.float32), 0.099609375, 1.8984375).astype(jnp.bfloat16),
        "second_shift": normal_values(splits[15], (D,), 0.3, 2.0, ((0, 32),)),
        "bias_table": normal_values(splits[16], (TABLE, HEADS), 1.0, 4.0),
        "cotangent": normal_values(splits[17], (SLOTS, HEIGHT, WIDTH, D), 1.0, 6.0, ((0, 8), (1, 2), (2, 2))),
    }


EPS = 1e-05
MASK_FILL = -100.0
PRECISE = lax.Precision.HIGHEST

@jax.custom_vjp
def low(v):
    return lax.optimization_barrier(v.astype(jnp.bfloat16)).astype(jnp.float32)

@jax.custom_vjp
def low_back(v):
    return v

def low_keep(v):
    return (low(v), None)

def low_pass(kept, grad):
    return (grad,)

def back_keep(v):
    return (v, None)

def back_low(kept, grad):
    return (low(grad),)
low.defvjp(low_keep, low_pass)
low_back.defvjp(back_keep, back_low)

def layer_norm(field, gain_vector, shift_vector):
    centred = field - lax.optimization_barrier(jnp.mean(field, axis=-1, keepdims=True))
    variance = lax.optimization_barrier(jnp.mean(centred * centred, axis=-1, keepdims=True))
    return centred * lax.rsqrt(variance + EPS) * gain_vector + shift_vector

def dense(field, matrix):
    return jnp.einsum('...d,de->...e', field, matrix, precision=PRECISE)

def to_windows(field):
    number = field.shape[0]
    channels = field.shape[-1]
    blocks = field.reshape(number, N_TH, WIN, N_TW, WIN, channels).transpose(0, 1, 3, 2, 4, 5)
    return blocks.reshape(number * N_TH * N_TW, WIN * WIN, channels)

def from_windows(blocks, number):
    channels = blocks.shape[-1]
    field = blocks.reshape(number, N_TH, N_TW, WIN, WIN, channels).transpose(0, 1, 3, 2, 4, 5)
    return field.reshape(number, N_TH * WIN, N_TW * WIN, channels)

def forward(images, keep_mask, params, region_ids, relative_index):
    entry_weight, entry_bias, exit_weight, exit_bias, expand_weight, expand_bias, reduce_weight, reduce_bias, first_gain, first_shift, second_gain, second_shift, bias_table = params
    number = images.shape[0]
    first = low_back(low(layer_norm(images, first_gain, first_shift)))
    rolled = jnp.roll(first, (-SHIFT, -SHIFT), axis=(1, 2))
    windows = to_windows(rolled)
    window_count = windows.shape[0]
    key_zeros = jnp.zeros((D,), jnp.float32)
    full_bias = jnp.concatenate([entry_bias[:D], key_zeros, entry_bias[D:]])
    triple = low_back(low(dense(windows, entry_weight) + full_bias))
    split_shape = (window_count, AREA, HEADS, HD)
    queries = triple[..., :D].reshape(split_shape)
    keys_part = triple[..., D:2 * D].reshape(split_shape)
    values_part = triple[..., 2 * D:].reshape(split_shape)
    region_win = to_windows(region_ids[None, :, :, None])[..., 0]
    mask_add = jnp.where(region_win[:, :, None] == region_win[:, None, :], 0.0, MASK_FILL).astype(jnp.float32)
    table_bias = jnp.take(bias_table, relative_index, axis=0).transpose(2, 0, 1)
    scores = jnp.einsum('nqhd,nkhd->nhqk', queries, keys_part, precision=PRECISE) * HD ** (-0.5)
    scores = scores.reshape(number, N_TH * N_TW, HEADS, AREA, AREA) + table_bias[None, None] + mask_add[None, :, None]
    scores = low_back(scores.reshape(window_count, HEADS, AREA, AREA))
    chances = low(jax.nn.softmax(scores, axis=-1))
    attended = jnp.einsum('nhqk,nkhd->nqhd', chances, values_part, precision=PRECISE).reshape(window_count, AREA, D)
    attended = low_back(low(attended))
    branch = low_back(low(dense(attended, exit_weight) + exit_bias))
    placed = jnp.roll(from_windows(branch, number), (SHIFT, SHIFT), axis=(1, 2))
    middle = images + placed
    second = low(layer_norm(middle, second_gain, second_shift))
    hidden = low_back(dense(second, expand_weight) + expand_bias)
    activated = low(jax.nn.gelu(hidden, approximate=False))
    feed_out = low_back(dense(activated, reduce_weight) + reduce_bias)
    return (middle + feed_out) * keep_mask[:, None, None, None]

def reference(images, valid_slots, region_ids, relative_index, entry_weight, entry_bias, exit_weight, exit_bias, expand_weight, expand_bias, reduce_weight, reduce_bias, first_gain, first_shift, second_gain, second_shift, bias_table, cotangent):
    params = tuple((member.astype(jnp.float32) for member in (entry_weight, entry_bias, exit_weight, exit_bias, expand_weight, expand_bias, reduce_weight, reduce_bias, first_gain, first_shift, second_gain, second_shift, bias_table)))
    group_size = math.gcd(SLOTS, 8)
    group_count = SLOTS // group_size
    grouped = (images.reshape((group_count, group_size) + images.shape[1:]), valid_slots.reshape(group_count, group_size), cotangent.reshape((group_count, group_size) + cotangent.shape[1:]))

    def one_group(carried, batch_item):
        inputs, keep_ints, grad_rows = batch_item
        keep_mask = keep_ints.astype(jnp.float32)

        def run_layer(image_values, weights):
            return forward(image_values, keep_mask, weights, region_ids, relative_index)
        result, pull_back = jax.vjp(run_layer, inputs.astype(jnp.float32), params)
        grad_in, grad_params = pull_back(grad_rows.astype(jnp.float32))
        carried = jax.tree.map(jnp.add, carried, grad_params)
        return (carried, (result.astype(jnp.bfloat16), grad_in.astype(jnp.bfloat16)))
    start = tuple((jnp.zeros_like(member) for member in params))
    sums, stacked = lax.scan(one_group, start, grouped)
    outputs, grads_in = stacked
    entry_grad, entry_bias_grad, exit_grad, exit_bias_grad, expand_grad, expand_bias_grad, reduce_grad, reduce_bias_grad, first_gain_grad, first_shift_grad, second_gain_grad, second_shift_grad, table_grad = sums
    return (outputs.reshape(images.shape), grads_in.reshape(images.shape), entry_grad, entry_bias_grad, exit_grad, exit_bias_grad, expand_grad, expand_bias_grad, reduce_grad, reduce_bias_grad, first_gain_grad, first_shift_grad, second_gain_grad, second_shift_grad, table_grad)
```

```python
import functools

import jax
import jax.numpy as jnp
from jax import lax
from jax.experimental import pallas as pl
from jax.experimental.pallas import tpu as pltpu
from jax.sharding import PartitionSpec as P

EPS = 1e-05
MASK_FILL = -100.0
HALF_ROOT = 0.7071067811865476
INV_ROOT_TAU = 0.3989422804014327
BF = jnp.bfloat16
F32 = jnp.float32
VMEM_BYTES = 60 << 20


def dot_nn(a, b):
    return lax.dot_general(a, b, (((1,), (0,)), ((), ())), preferred_element_type=F32)


def dot_nt(a, b):
    return lax.dot_general(a, b, (((1,), (1,)), ((), ())), preferred_element_type=F32)


def dot_tn(a, b):
    return lax.dot_general(a, b, (((0,), (0,)), ((), ())), preferred_element_type=F32)


def swap(value, axis, mask):
    count = lax.axis_size(axis)
    return lax.ppermute(value, axis, [(i, i ^ mask) for i in range(count)])


def pick(value, index):
    return lax.dynamic_index_in_dim(value, index, 0, keepdims=False)


def params(**kw):
    return pltpu.CompilerParams(vmem_limit_bytes=VMEM_BYTES, **kw)


def cost(flops, nbytes, trans=0):
    return pl.CostEstimate(flops=int(flops), bytes_accessed=int(nbytes), transcendentals=int(trans))


def place_kernel(widths, rows, fold, order_ref, mine_ref, theirs_ref, *outs):
    core = order_ref[order_ref.shape[0] - 1]
    own = mine_ref[0]
    other = theirs_ref[0]
    first = jnp.where(core == 0, own, other)
    second = jnp.where(core == 0, other, own)
    at = 0
    for out, width, parts in zip(outs, widths, fold):
        for part in range(parts):
            out[part * rows : (part + 1) * rows, :] = first[:, at : at + width]
            out[(parts + part) * rows : (parts + part + 1) * rows, :] = second[:, at : at + width]
            at += width


def gather_blocks(block, widths, fold, y_first):
    rows = block.shape[0]
    batch, high, core = (lax.axis_index(a) for a in ("batch", "th", "tw"))
    held = jnp.stack([block] + [swap(block, "batch", m << 1) for m in (1, 2, 3)])
    steps = [("th", 1), ("batch", 1)] if y_first else [("batch", 1), ("th", 1)]
    for axis, mask in steps:
        held = jnp.concatenate([held, swap(held, axis, mask)])
    theirs = swap(held, "tw", 1)
    chips = held.shape[0]
    target = jnp.arange(chips, dtype=jnp.int32) ^ (batch * 2 + high).astype(jnp.int32)
    y_bit, x_bit, z_bits = target & 1, (target >> 1) & 1, target >> 2
    low, top = (y_bit, x_bit) if y_first else (x_bit, y_bit)
    order = jnp.concatenate([top * 8 + low * 4 + z_bits, core.astype(jnp.int32)[None]])
    shapes = [(chips * 2 * rows * f, w) for w, f in zip(widths, fold)]
    return pl.pallas_call(
        functools.partial(place_kernel, widths, rows, fold),
        grid_spec=pltpu.PrefetchScalarGridSpec(
            num_scalar_prefetch=1,
            grid=(chips,),
            in_specs=[pl.BlockSpec((1,) + block.shape, lambda c, o: (o[c], 0, 0))] * 2,
            out_specs=[pl.BlockSpec((2 * rows * f, w), lambda c, o: (c, 0)) for w, f in zip(widths, fold)],
        ),
        out_shape=[jax.ShapeDtypeStruct(s, block.dtype) for s in shapes],
        compiler_params=params(),
        cost_estimate=cost(0, 4 * chips * block.size * 2),
        name="place",
    )(order, held, theirs)


def scatter_sum(whole, rows, y_first):
    batch, high, core = (lax.axis_index(a) for a in ("batch", "th", "tw"))
    width = whole.shape[1]
    kept = whole.reshape(-1, 2, rows, width).swapaxes(0, 1)
    got = swap(pick(kept, 1 - core), "tw", 1)
    kept = pick(kept, core).astype(F32) + got.astype(F32)
    kept = kept.reshape(-1, 2, 2, rows, width)
    kept = kept.transpose(2, 1, 0, 3, 4)
    if not y_first:
        kept = kept.swapaxes(0, 1)
    x_bit = batch & 1
    plan = [("th", high), ("batch", x_bit)] if y_first else [("batch", x_bit), ("th", high)]
    for axis, bit in plan:
        got = swap(pick(kept, 1 - bit).astype(BF), axis, 1)
        kept = pick(kept, bit) + got.astype(F32)
    spot = batch >> 1
    total = pick(kept, spot)
    for mask in (1, 2, 3):
        total = total + swap(pick(kept, spot ^ mask).astype(BF), "batch", mask << 1).astype(F32)
    return total


def sum_everywhere(value):
    value = value + swap(value, "tw", 1)
    value = value + swap(value, "th", 1)
    step = 1
    while step < lax.axis_size("batch"):
        value = value + swap(value, "batch", step)
        step *= 2
    return value


def tiles_to_images(tiles):
    high, core = lax.axis_index("th"), lax.axis_index("tw")
    side, width = tiles.shape[1], tiles.shape[3]
    half = side // 2
    split = tiles.reshape((2, 2, -1) + tiles.shape[1:])
    own = pick(split, high)
    got = swap(pick(split, 1 - high), "th", 1)
    rows = jnp.where(high == 0, jnp.stack([own, got]), jnp.stack([got, own]))
    rows = rows.swapaxes(0, 1)
    own = pick(rows, core)
    got = swap(pick(rows, 1 - core), "tw", 1)
    grid = jnp.where(core == 0, jnp.stack([own, got]), jnp.stack([got, own]))
    grid = grid.transpose(2, 1, 3, 0, 4, 5).reshape(-1, 2 * side, 2 * side, width)
    grid = jnp.roll(grid, (-half, -half), axis=(1, 2))
    return grid.reshape(-1, 2, side, 2, side, width).transpose(0, 1, 3, 2, 4, 5)


def images_to_tiles(windows):
    high, core = lax.axis_index("th"), lax.axis_index("tw")
    count, side, width = windows.shape[0], windows.shape[3], windows.shape[5]
    half = side // 2
    grid = windows.transpose(0, 1, 3, 2, 4, 5).reshape(count, 2 * side, 2 * side, width)
    grid = jnp.roll(grid, (half, half), axis=(1, 2))
    grid = grid.reshape(count, 2, side, 2, side, width).transpose(3, 1, 0, 2, 4, 5)
    own = pick(grid, core)
    got = swap(pick(grid, 1 - core), "tw", 1)
    rows = jnp.where(core == 0, jnp.stack([own, got]), jnp.stack([got, own]))
    rows = rows.swapaxes(0, 1)
    own = pick(rows, high)
    got = swap(pick(rows, 1 - high), "th", 1)
    tiles = jnp.where(high == 0, jnp.stack([own, got]), jnp.stack([got, own]))
    return tiles.reshape((-1, side, side, width))


def look_kernel(index_ref, table_ref, out_ref):
    entries = table_ref.shape[1]
    for k in range(index_ref.shape[0]):
        spots = index_ref[k : k + 1, :]
        level = lax.broadcasted_iota(jnp.int32, (entries, spots.shape[1]), 0)
        hot = jnp.where(level == spots, 1.0, 0.0).astype(BF)
        out_ref[k] = dot_nn(table_ref[...], hot)


def look_up(table_t, index_t, step):
    area = index_t.shape[0]
    heads, entries = table_t.shape
    return pl.pallas_call(
        look_kernel,
        grid=(area // step,),
        in_specs=[
            pl.BlockSpec((step, area), lambda i: (i, 0)),
            pl.BlockSpec((heads, entries), lambda i: (0, 0)),
        ],
        out_specs=pl.BlockSpec((step, heads, area), lambda i: (i, 0, 0)),
        out_shape=jax.ShapeDtypeStruct((area, heads, area), F32),
        compiler_params=params(),
        cost_estimate=cost(2 * 256 * entries * area * area, area * area * heads * 4),
        name="look",
    )(index_t, table_t)


def count_kernel(index_ref, grad_ref, out_ref):
    @pl.when(pl.program_id(0) == 0)
    def _():
        out_ref[...] = jnp.zeros_like(out_ref)

    entries = out_ref.shape[0]
    total = jnp.zeros(out_ref.shape, F32)
    for k in range(index_ref.shape[0]):
        spots = index_ref[k : k + 1, :]
        level = lax.broadcasted_iota(jnp.int32, (entries, spots.shape[1]), 0)
        hot = jnp.where(level == spots, 1.0, 0.0).astype(BF)
        total = total + dot_nt(hot, grad_ref[k])
    out_ref[...] += total


def count_up(grads, index_t, entries, step):
    area, columns, _ = grads.shape
    return pl.pallas_call(
        count_kernel,
        grid=(area // step,),
        in_specs=[
            pl.BlockSpec((step, area), lambda i: (i, 0)),
            pl.BlockSpec((step, columns, area), lambda i: (i, 0, 0)),
        ],
        out_specs=pl.BlockSpec((entries, columns), lambda i: (0, 0)),
        out_shape=jax.ShapeDtypeStruct((entries, columns), F32),
        compiler_params=params(),
        cost_estimate=cost(2 * 256 * entries * area * area, grads.size * 2),
        name="count",
    )(index_t, grads)


def lanes_of(shape, head, size):
    lane = lax.broadcasted_iota(jnp.int32, shape, 1)
    return (lane >= head * size) & (lane < (head + 1) * size)


def attend_kernel(width, size, triple_ref, bias_ref, mask_ref, out_ref, lse_ref):
    scale = size ** (-0.5)
    per = 128 // size
    area = triple_ref.shape[1]
    wall = mask_ref[0]

    def group(g, carry):
        at = pl.multiple_of(g * 128, 128)
        queries = triple_ref[0, :, pl.ds(at, 128)]
        keys = triple_ref[0, :, pl.ds(pl.multiple_of(width + at, 128), 128)]
        values = triple_ref[0, :, pl.ds(pl.multiple_of(2 * width + at, 128), 128)]
        values_t = values.astype(F32).T.astype(BF)
        found = []
        for i in range(per):
            own = lanes_of((area, 128), i, size)
            head = g * per + i
            scores = dot_nt(jnp.where(own, keys, jnp.zeros_like(keys)), queries) * scale
            scores = scores + (bias_ref[head] + wall)
            top = jnp.max(scores, axis=0, keepdims=True)
            raised = jnp.exp(scores - top)
            total = jnp.sum(raised, axis=0, keepdims=True)
            chances = (raised * (1.0 / total)).astype(BF)
            lse_ref[0, pl.ds(head, 1), :] = top + jnp.log(total)
            found.append(dot_nn(values_t[i * size : (i + 1) * size, :], chances))
        out_ref[0, :, pl.ds(at, 128)] = jnp.concatenate(found, axis=0).T.astype(BF)
        return carry

    lax.fori_loop(0, width // 128, group, 0)


def attend(triple, bias, masks, size):
    count, area, wide = triple.shape
    width = wide // 3
    heads = bias.shape[0]
    per_image = masks.shape[0]
    return pl.pallas_call(
        functools.partial(attend_kernel, width, size),
        grid=(count,),
        in_specs=[
            pl.BlockSpec((1, area, wide), lambda i: (i, 0, 0)),
            pl.BlockSpec((heads, area, area), lambda i: (0, 0, 0)),
            pl.BlockSpec((1, area, area), lambda i: (i % per_image, 0, 0)),
        ],
        out_specs=[
            pl.BlockSpec((1, area, width), lambda i: (i, 0, 0)),
            pl.BlockSpec((1, heads, area), lambda i: (i, 0, 0)),
        ],
        out_shape=[
            jax.ShapeDtypeStruct((count, area, width), BF),
            jax.ShapeDtypeStruct((count, heads, area), F32),
        ],
        compiler_params=params(),
        cost_estimate=cost(count * heads * area * area * 4 * 256, triple.size * 3, count * heads * area * area),
        name="attend",
    )(triple, bias, masks)


def attend_back_kernel(width, size, triple_ref, given_ref, bias_ref, mask_ref, lse_ref, out_ref, total_ref):
    scale = size ** (-0.5)
    per = 128 // size
    area = triple_ref.shape[1]
    wall = mask_ref[0]

    @pl.when(pl.program_id(0) == 0)
    def _():
        total_ref[...] = jnp.zeros_like(total_ref)

    def group(g, carry):
        at = pl.multiple_of(g * 128, 128)
        queries = triple_ref[0, :, pl.ds(at, 128)]
        keys = triple_ref[0, :, pl.ds(pl.multiple_of(width + at, 128), 128)]
        values = triple_ref[0, :, pl.ds(pl.multiple_of(2 * width + at, 128), 128)]
        given = given_ref[0, :, pl.ds(at, 128)]
        keys_t = keys.astype(F32).T.astype(BF)
        zero = jnp.zeros_like(keys)
        to_queries = []
        to_keys = jnp.zeros((area, 128), F32)
        to_values = jnp.zeros((area, 128), F32)
        for i in range(per):
            own = lanes_of((area, 128), i, size)
            head = g * per + i
            scores = dot_nt(jnp.where(own, keys, zero), queries) * scale
            scores = scores + (bias_ref[head] + wall)
            chances = jnp.exp(scores - lse_ref[0, pl.ds(head, 1), :])
            to_values = to_values + dot_nn(chances.astype(BF), jnp.where(own, given, zero))
            slopes = dot_nt(jnp.where(own, values, zero), given)
            scaled = chances * slopes
            delta = jnp.sum(scaled, axis=0, keepdims=True)
            moved = (scaled - chances * delta).astype(BF)
            total_ref[head] += moved.astype(F32)
            to_keys = to_keys + dot_nn(moved, jnp.where(own, queries, zero))
            to_queries.append(dot_nn(keys_t[i * size : (i + 1) * size, :], moved))
        out_ref[0, :, pl.ds(at, 128)] = (jnp.concatenate(to_queries, axis=0).T * scale).astype(BF)
        out_ref[0, :, pl.ds(pl.multiple_of(width + at, 128), 128)] = (to_keys * scale).astype(BF)
        out_ref[0, :, pl.ds(pl.multiple_of(2 * width + at, 128), 128)] = to_values.astype(BF)
        return carry

    lax.fori_loop(0, width // 128, group, 0)


def attend_back(triple, given, bias, masks, lse, size):
    count, area, wide = triple.shape
    width = wide // 3
    heads = bias.shape[0]
    per_image = masks.shape[0]
    return pl.pallas_call(
        functools.partial(attend_back_kernel, width, size),
        grid=(count,),
        in_specs=[
            pl.BlockSpec((1, area, wide), lambda i: (i, 0, 0)),
            pl.BlockSpec((1, area, width), lambda i: (i, 0, 0)),
            pl.BlockSpec((heads, area, area), lambda i: (0, 0, 0)),
            pl.BlockSpec((1, area, area), lambda i: (i % per_image, 0, 0)),
            pl.BlockSpec((1, heads, area), lambda i: (i, 0, 0)),
        ],
        out_specs=[
            pl.BlockSpec((1, area, wide), lambda i: (i, 0, 0)),
            pl.BlockSpec((heads, area, area), lambda i: (0, 0, 0)),
        ],
        out_shape=[
            jax.ShapeDtypeStruct((count, area, wide), BF),
            jax.ShapeDtypeStruct((heads, area, area), F32),
        ],
        compiler_params=params(),
        cost_estimate=cost(count * heads * area * area * 10 * 256, triple.size * 6, count * heads * area * area),
        name="attend_back",
    )(triple, given, bias, masks, lse)


def feed_kernel(tile, second_ref, given_ref, up_ref, up_bias_ref, down_ref,
                out_ref, back_ref, up_grad_ref, down_grad_ref, bias_grad_ref, active_ref, moved_ref):
    first = pl.program_id(0) == 0

    @pl.when(first)
    def _():
        out_ref[...] = jnp.zeros_like(out_ref)
        back_ref[...] = jnp.zeros_like(back_ref)

    bias_grad_ref[...] = jnp.zeros_like(bias_grad_ref)

    def part(r, carry):
        rows = pl.ds(pl.multiple_of(r * tile, tile), tile)
        hidden = dot_nn(second_ref[rows, :], up_ref[...]) + up_bias_ref[...]
        chance = 0.5 * (1.0 + lax.erf(hidden * HALF_ROOT))
        active = (hidden * chance).astype(BF)
        slope = chance + hidden * INV_ROOT_TAU * jnp.exp(-0.5 * hidden * hidden)
        moved = (dot_nt(given_ref[rows, :], down_ref[...]) * slope).astype(BF)
        active_ref[rows, :] = active
        moved_ref[rows, :] = moved
        bias_grad_ref[...] += jnp.sum(moved.astype(F32), axis=0, keepdims=True)
        out_ref[rows, :] += dot_nn(active, down_ref[...])
        back_ref[rows, :] += dot_nt(moved, up_ref[...])
        return carry

    lax.fori_loop(0, second_ref.shape[0] // tile, part, 0)
    down_grad_ref[...] = dot_tn(active_ref[...], given_ref[...]).astype(BF)
    up_grad_ref[...] = dot_tn(second_ref[...], moved_ref[...]).astype(BF)


def feed(second, given, up, up_bias, down, chunk=512, tile=288):
    tokens, width = second.shape
    hidden = up.shape[1]
    fixed = pl.BlockSpec((tokens, width), lambda j: (0, 0), pipeline_mode=pl.Buffered(1))
    return pl.pallas_call(
        functools.partial(feed_kernel, tile),
        grid=(hidden // chunk,),
        in_specs=[
            fixed,
            fixed,
            pl.BlockSpec((width, chunk), lambda j: (0, j)),
            pl.BlockSpec((1, chunk), lambda j: (0, j)),
            pl.BlockSpec((chunk, width), lambda j: (j, 0)),
        ],
        out_specs=[
            pl.BlockSpec((tokens, width), lambda j: (0, 0)),
            pl.BlockSpec((tokens, width), lambda j: (0, 0)),
            pl.BlockSpec((width, chunk), lambda j: (0, j)),
            pl.BlockSpec((chunk, width), lambda j: (j, 0)),
            pl.BlockSpec((1, chunk), lambda j: (0, j)),
        ],
        out_shape=[
            jax.ShapeDtypeStruct((tokens, width), F32),
            jax.ShapeDtypeStruct((tokens, width), F32),
            jax.ShapeDtypeStruct((width, hidden), BF),
            jax.ShapeDtypeStruct((hidden, width), BF),
            jax.ShapeDtypeStruct((1, hidden), F32),
        ],
        scratch_shapes=[pltpu.VMEM((tokens, chunk), BF), pltpu.VMEM((tokens, chunk), BF)],
        compiler_params=params(),
        cost_estimate=cost(12 * tokens * width * hidden, 16 * width * hidden, 2 * tokens * hidden),
        name="feed",
    )(second, given, up, up_bias, down)


def norm_forward(field, gain_vector, shift_vector):
    centred = field - jnp.mean(field, axis=-1, keepdims=True)
    inverse = lax.rsqrt(jnp.mean(centred * centred, axis=-1, keepdims=True) + EPS)
    normed = centred * inverse
    return (normed * gain_vector + shift_vector, normed, inverse)


def norm_backward(grad_rows, normed, inverse, gain_vector):
    scaled = grad_rows * gain_vector
    first_mean = jnp.mean(scaled, axis=-1, keepdims=True)
    second_mean = jnp.mean(scaled * normed, axis=-1, keepdims=True)
    grad_field = inverse * (scaled - first_mean - normed * second_mean)
    return (grad_field, jnp.sum(grad_rows * normed, axis=0), jnp.sum(grad_rows, axis=0))


def body(
    images,
    valid_slots,
    region_ids,
    relative_index,
    entry_weight,
    entry_bias,
    exit_weight,
    exit_bias,
    expand_weight,
    expand_bias,
    reduce_weight,
    reduce_bias,
    first_gain,
    first_shift,
    second_gain,
    second_shift,
    bias_table,
    cotangent,
):
    every = ("batch", "th", "tw")
    side, width = images.shape[1], images.shape[3]
    area = side * side
    heads = bias_table.shape[1]
    size = width // heads
    rows = entry_weight.shape[0]
    devices = lax.axis_size("batch") * lax.axis_size("th") * lax.axis_size("tw")
    fan = reduce_weight.shape[0] // rows
    paired = rows % 8 == 0 and lax.axis_size("batch") == 8
    high, core, spot = lax.axis_index("th"), lax.axis_index("tw"), lax.axis_index("batch")
    owner = high * 2 + core

    smalls = (entry_bias, exit_bias, expand_bias, reduce_bias, first_gain, first_shift, second_gain, second_shift)
    small_cols = [s.shape[0] // rows for s in smalls]
    packed = jnp.concatenate([s.reshape(rows, -1) for s in smalls], axis=1)
    packed = jnp.pad(packed, ((0, 0), (0, 128 - packed.shape[1])))
    if paired:
        weight_entry, packed_full = gather_blocks(
            jnp.concatenate([entry_weight, packed], axis=1), (entry_weight.shape[1], 128), (1, 1), False
        )
    else:
        weight_entry = lax.all_gather(entry_weight, every, axis=0, tiled=True)
        packed_full = lax.all_gather(packed, every, axis=0, tiled=True)
    vectors = []
    at = 0
    for columns in small_cols:
        vectors.append(packed_full[:, at : at + columns].reshape(-1).astype(F32))
        at += columns
    (bias_entry, bias_exit, bias_expand, bias_reduce, gain_first, shift_first, gain_second, shift_second) = vectors

    image_windows = tiles_to_images(images)
    shape = image_windows.shape
    count = shape[0] * 4
    flat_low = image_windows.reshape(-1, width)

    if paired:
        reduce_cols = jnp.concatenate([reduce_weight[i * rows : (i + 1) * rows] for i in range(fan)], axis=1)
        weight_exit, weight_expand, weight_reduce = gather_blocks(
            jnp.concatenate([exit_weight, expand_weight, reduce_cols], axis=1),
            (width, expand_weight.shape[1], width),
            (1, 1, fan),
            True,
        )
    else:
        weight_exit = lax.all_gather(exit_weight, every, axis=0, tiled=True)
        weight_expand = lax.all_gather(expand_weight, every, axis=0, tiled=True)
        weight_reduce = lax.all_gather(reduce_weight, every, axis=0, tiled=True)
    given_windows = tiles_to_images(cotangent)

    entries = -(-bias_table.shape[0] // 128) * 128
    table_t = jnp.pad(bias_table, ((0, entries - bias_table.shape[0]), (0, 0))).T
    index_t = relative_index.T
    bias = look_up(table_t, index_t, 8).swapaxes(0, 1)
    region_flat = region_ids.reshape(1, area)
    region_rows = jnp.concatenate([region_flat, swap(region_flat, "tw", 1)])
    region_rows = jnp.where(core == 0, region_rows, region_rows[::-1])[None]
    region_all = jnp.concatenate([region_rows, swap(region_rows, "th", 1)])
    region_all = jnp.where(high == 0, region_all, region_all[::-1]).reshape(4, area)
    masks = jnp.where(region_all[:, :, None] == region_all[:, None, :], 0.0, MASK_FILL).astype(F32)

    flat_in = flat_low.astype(F32)
    normed_first, hat_first, inv_first = norm_forward(flat_in, gain_first, shift_first)
    windows = normed_first.astype(BF)
    full_bias = jnp.concatenate([bias_entry[:width], jnp.zeros((width,), F32), bias_entry[width:]])
    triple = (dot_nn(windows, weight_entry) + full_bias).astype(BF).reshape(count, area, 3 * width)
    attended, lse = attend(triple, bias, masks, size)
    attended = attended.reshape(-1, width)
    branch = (dot_nn(attended, weight_exit) + bias_exit).astype(BF)
    middle = flat_in + branch.astype(F32)
    normed_second, hat_second, inv_second = norm_forward(middle, gain_second, shift_second)
    second_low = normed_second.astype(BF)
    keep = lax.dynamic_slice_in_dim(valid_slots, owner * shape[0], shape[0]).astype(F32)
    keep_rows = jnp.repeat(keep, 4 * area)[:, None]
    grad_out = given_windows.reshape(-1, width).astype(F32) * keep_rows
    grad_feed = grad_out.astype(BF)
    feed_out, grad_second, up_grad, down_grad, up_bias_grad = feed(
        second_low, grad_feed, weight_expand, bias_expand[None], weight_reduce
    )
    result = ((middle + feed_out + bias_reduce) * keep_rows).astype(BF)
    output = images_to_tiles(result.reshape(shape))

    grad_middle, second_gain_part, second_shift_part = norm_backward(grad_second, hat_second, inv_second, gain_second)
    grad_middle = grad_out + grad_middle
    grad_branch = grad_middle.astype(BF)
    exit_grad = dot_tn(attended, grad_branch).astype(BF)
    grad_attended = dot_nt(grad_branch, weight_exit).astype(BF).reshape(count, area, width)
    grad_triple, moved_total = attend_back(triple, grad_attended, bias, masks, lse, size)
    grad_triple = grad_triple.reshape(-1, 3 * width)
    entry_grad = dot_tn(windows, grad_triple).astype(BF)
    grad_first = dot_nt(grad_triple, weight_entry).astype(BF).astype(F32)
    grad_input, first_gain_part, first_shift_part = norm_backward(grad_first, hat_first, inv_first, gain_first)
    images_grad = images_to_tiles((grad_input + grad_middle).astype(BF).reshape(shape))

    spread = moved_total.swapaxes(0, 1)
    spread_high = spread.astype(BF)
    spread_low = (spread - spread_high.astype(F32)).astype(BF)
    table_part = count_up(jnp.concatenate([spread_high, spread_low], axis=1), index_t, entries, 8)
    table_part = table_part[: bias_table.shape[0], :heads] + table_part[: bias_table.shape[0], heads:]

    column_sums = jnp.sum(grad_triple.astype(F32), axis=0)
    small_parts = [
        column_sums[:width],
        column_sums[2 * width :],
        jnp.sum(grad_branch.astype(F32), axis=0),
        up_bias_grad[0],
        jnp.sum(grad_feed.astype(F32), axis=0),
        first_gain_part,
        first_shift_part,
        second_gain_part,
        second_shift_part,
    ]
    lane = 128
    flat_parts = jnp.concatenate(small_parts + [table_part.reshape(-1)])
    length = flat_parts.shape[0]
    padded = -(-length // (8 * lane)) * 8 * lane
    summed = sum_everywhere(jnp.pad(flat_parts, (0, padded - length)).reshape(-1, lane)).reshape(-1)
    here = (spot * 2 + high) * 2 + core
    small_outs = []
    at = 0
    for small in smalls:
        part = small.shape[0]
        small_outs.append(lax.dynamic_slice_in_dim(summed, at + here * part, part))
        at += part * devices
    (entry_bias_out, exit_bias_out, expand_bias_out, reduce_bias_out, *norm_outs) = small_outs
    table_grad = summed[at : at + bias_table.size].reshape(bias_table.shape)

    if paired:
        down_out = scatter_sum(down_grad, rows * fan, True)
        up_out = scatter_sum(up_grad, rows, False)
        exit_out = scatter_sum(exit_grad, rows, True)
        entry_out = scatter_sum(entry_grad, rows, False)
    else:
        entry_out, exit_out, up_out, down_out = (
            lax.psum_scatter(g.astype(F32), every, scatter_dimension=0, tiled=True)
            for g in (entry_grad, exit_grad, up_grad, down_grad)
        )
    return (
        output,
        images_grad,
        entry_out,
        entry_bias_out,
        exit_out,
        exit_bias_out,
        up_out,
        expand_bias_out,
        down_out,
        reduce_bias_out,
        *norm_outs,
        table_grad,
    )


def solution(mesh):
    every = ("batch", "th", "tw")
    tiles = P("batch", "th", "tw", None)
    matrix, vector = P(every, None), P(every)
    in_specs = (tiles, P("batch"), P("th", "tw"), P()) + (matrix, vector) * 4 + (vector,) * 4 + (P(), tiles)
    out_specs = (tiles, tiles) + (matrix, vector) * 4 + (vector,) * 4 + (P(),)
    return jax.shard_map(body, mesh=mesh, in_specs=in_specs, out_specs=out_specs, check_vma=False)
```
